768 devices in a mesh: ctx: 16 (over y_hi, x), ch: 48 (over z, y_lo, core).
Axes of the slice: x: 4, y: 8 (y_hi: 4, y_lo: 2; y = y_hi * 2 + y_lo), z: 12, core: 2. Of those that a mesh axis runs over, the one named last changes fastest.
Arguments:
- tokens_in: bfloat16 [12288, 4096], P('ctx'), may hold values from -6 to 6
- w_in: bfloat16 [4096, 3, 3072], P(None, None, 'ch'), may hold values from -0.09375 to 0.09375
- filter_bank: bfloat16 [24, 16, 256], replicated, may hold values from -0.09375 to 0.09375
- lag_blocks: int32 [24, 32], replicated, may hold values from 0 to 95, as said below
- filter_ids: int32 [24, 32], replicated, may hold values from 0 to 15
- grad_out: bfloat16 [3072, 12288], P('ch', 'ctx'), may hold values from -0.019897461 to 0.019897461
Outputs:
- gated_out: bfloat16 [3072, 12288], P('ch', 'ctx')
- w_grad: float32 [4096, 3, 3072], P('ctx', None, 'ch')
- filter_grad: float32 [24, 16, 256], replicated
The draws below stay inside these ranges and needn't reach their ends.
Inputs may be any that keep to these rules, and one draw needn't show every extreme that they name: `lag_blocks`: in each group's row the 32 lags are distinct and the first is 0; row 0 lists the lag 96 - 1.
All inputs are finite; a program needn't handle non-finite values.
Results may differ from the reference program's by a relative error of at most 0.0058.
The reference program's roundings to bfloat16 on the way count: a program that leaves them out, or rounds other values in their place, can miss the bound.
Values may be sent and summed in bfloat16 or wider, within the bound.
No kernel may reach another device: no remote copies, remote signals or barrier semaphores. Data moves between devices by JAX's collectives and lax.ppermute only.
A program may use at most 64 MiB of HBM per device.

```python
import jax
import jax.numpy as jnp
from jax import lax

D = 4096
C = 3072
GROUP = 128
G = 24
BLK = 128
TOKENS = 12288
NBLK = 96
K = 32
NF = 16


def draw_lag_blocks(key, part):
    row_keys = jax.random.split(jax.random.fold_in(key, 7), G)

    def one_row(row_key, row_number):
        ordering = jax.random.permutation(row_key, NBLK - 1) + 1
        leading = ordering[0]
        swapped = jnp.where(ordering == NBLK - 1, leading, ordering)
        swapped = swapped.at[0].set(NBLK - 1)
        chosen = jnp.where(row_number == 0, swapped, ordering)
        return chosen[:K - 1]
    remaining = jax.vmap(one_row)(row_keys, jnp.arange(G))
    return jnp.concatenate([jnp.zeros((G, 1), jnp.int32), remaining.astype(jnp.int32)], axis=1)


def with_ends(values, stream_key, least, largest):
    dims = values.shape
    index_at = [jax.random.randint(jax.random.fold_in(stream_key, axis), (), 0, dims[axis]) for axis in range(len(dims))]
    values = values.at[tuple(index_at)].set(least)
    longest = dims.index(max(dims))
    index_at[longest] = (index_at[longest] + 1) % dims[longest]
    return values.at[tuple(index_at)].set(largest)


def steps_of(key, dims, cuts, low, largest):
    loudness = 1.0
    for position, shards_of in cuts:
        heights = jax.random.uniform(jax.random.fold_in(jax.random.fold_in(key, 6), position), (shards_of,), jnp.float32, low / len(cuts), largest / len(cuts))
        loudness = loudness * jnp.repeat(jnp.exp(heights), dims[position] // shards_of).reshape((-1,) + (1,) * (len(dims) - 1 - position))
    return loudness


def bell_draw(key, shape, spread, most, shards=(), held_as=jnp.bfloat16):
    factor_of = steps_of(key, shape, shards, -0.22, 0.18) if shards else 1.0
    drawn = jax.random.normal(key, shape, jnp.float32) * spread * factor_of
    return jnp.minimum(jnp.maximum(drawn, -most), most).astype(held_as)


def setup_inputs(seed: int = 0) -> dict:
    arg_keys = jax.random.split(jax.random.key(seed), 7)
    return {
        "tokens_in": bell_draw(arg_keys[0], (TOKENS, D), 1.0, 6.0, ((0, 16),)),
        "w_in": bell_draw(arg_keys[1], (D, 3, C), D ** -0.5, 0.09375, ((2, 48),)),
        "filter_bank": bell_draw(arg_keys[2], (G, NF, 2 * BLK), (K * BLK) ** -0.5, 0.09375),
        "lag_blocks": draw_lag_blocks(jax.random.fold_in(arg_keys[6], 71), 0),
        "filter_ids": with_ends(jax.random.randint(arg_keys[4], (G, K), 0, NF), jax.random.fold_in(arg_keys[4], 1), 0, NF - 1).astype(jnp.int32),
        "grad_out": bell_draw(arg_keys[5], (C, TOKENS), 0.003, 0.019897461, ((0, 48), (1, 16))),
    }


def toeplitz(filter_taps, lag_list):
    row_index = jnp.arange(BLK)[:, None]
    col_index = jnp.arange(BLK)[None, :]
    matrices = filter_taps[:, BLK + row_index - col_index]
    upper = (row_index < col_index)[None, :, :] & (lag_list == 0)[:, None, None]
    return jnp.where(upper, jnp.zeros_like(matrices), matrices)


def per_group(group_items):
    streams, cot_group, group_bank, lag_list, id_list = group_items
    outer = streams[0].astype(jnp.float32)
    inner = streams[1].astype(jnp.float32)
    values = streams[2].astype(jnp.float32)
    mixed = (inner * values).astype(jnp.bfloat16)
    grad_conv = (cot_group.astype(jnp.float32) * outer).astype(jnp.bfloat16)
    filter_taps = group_bank[id_list]
    matrices = toeplitz(filter_taps, lag_list)
    earlier = jnp.concatenate([jnp.zeros_like(mixed), mixed], axis=1)
    later_pad = jnp.concatenate([grad_conv, jnp.zeros_like(grad_conv)], axis=1)
    conv_rows = grad_conv.reshape(GROUP * NBLK, BLK)

    def lag_step(running, lag_entry):
        conv_out, grad_mixed = running
        lag_value, matrix = lag_entry
        shift = (lag_value * BLK).astype(jnp.int32)
        window = lax.dynamic_slice_in_dim(earlier, (TOKENS - shift).astype(jnp.int32), TOKENS, 1)
        ahead_rows = lax.dynamic_slice_in_dim(later_pad, shift, TOKENS, 1)
        window_rows = window.reshape(GROUP * NBLK, BLK)
        conv_out = conv_out + jnp.dot(window_rows, matrix.T, preferred_element_type=jnp.float32).reshape(GROUP, TOKENS)
        grad_mixed = grad_mixed + jnp.dot(ahead_rows.reshape(GROUP * NBLK, BLK), matrix, preferred_element_type=jnp.float32).reshape(GROUP, TOKENS)
        grad_mat = jnp.dot(conv_rows.T, window_rows, preferred_element_type=jnp.float32)
        return (conv_out, grad_mixed), grad_mat

    empty_field = jnp.zeros((GROUP, TOKENS), jnp.float32)
    (conv_out, grad_mixed), grad_mats = lax.scan(lag_step, (empty_field, empty_field), (lag_list, matrices))
    row_index = jnp.arange(BLK)[:, None]
    col_index = jnp.arange(BLK)[None, :]
    upper = (row_index < col_index)[None, :, :] & (lag_list == 0)[:, None, None]
    grad_mats = jnp.where(upper, jnp.zeros_like(grad_mats), grad_mats)
    offsets = (BLK + row_index - col_index).reshape(-1)
    grad_taps = jnp.zeros((K, 2 * BLK), jnp.float32).at[:, offsets].add(grad_mats.reshape(K, BLK * BLK))
    onehot = (id_list[:, None] == jnp.arange(NF)[None, :]).astype(jnp.float32)
    group_table = jnp.dot(onehot.T, grad_taps, precision=lax.Precision.HIGHEST)
    gated_group = (outer * conv_out).astype(jnp.bfloat16)
    grad_first = cot_group.astype(jnp.float32) * conv_out
    grad_second = grad_mixed * values
    grad_third = grad_mixed * inner
    grad_group = jnp.stack([grad_first, grad_second, grad_third]).astype(jnp.bfloat16)
    return gated_group, grad_group, group_table


def reference(tokens_in, w_in, filter_bank, lag_blocks, filter_ids, grad_out):
    flat_proj = jnp.dot(tokens_in, w_in.reshape(D, 3 * C), preferred_element_type=jnp.float32).astype(jnp.bfloat16)
    projected = jnp.transpose(flat_proj.reshape(TOKENS, 3, C), (1, 2, 0))
    grouped = jnp.transpose(projected.reshape(3, G, GROUP, TOKENS), (1, 0, 2, 3))
    cotangent = grad_out.reshape(G, GROUP, TOKENS)
    gated_parts, grad_parts, filter_grad = lax.map(per_group, (grouped, cotangent, filter_bank, lag_blocks, filter_ids))
    gated_out = gated_parts.reshape(C, TOKENS)
    grad_flat = jnp.transpose(grad_parts, (1, 0, 2, 3)).reshape(3 * C, TOKENS)
    w_grad = jnp.dot(tokens_in.T, grad_flat.T, preferred_element_type=jnp.float32).reshape(D, 3, C)
    return gated_out, w_grad, filter_grad
```

```python
import jax
import jax.numpy as jnp
from jax import lax
from jax.experimental import pallas as pl
from jax.experimental.pallas import tpu as pltpu
from jax.sharding import PartitionSpec as P

BLK = 128
HALF = 4
BF16, F32 = jnp.bfloat16, jnp.float32


def low_rows(shape):
    return lax.broadcasted_iota(jnp.int32, shape, len(shape) - 2) < HALF


def project_kernel(w_ref, tok_ref, cot_ref, proj_ref, send_ref):
    chan = cot_ref.shape[0]
    width = tok_ref.shape[0]
    proj = lax.dot_general(
        w_ref[...], tok_ref[...], (((1,), (1,)), ((), ())), preferred_element_type=F32
    ).astype(BF16)
    proj_ref[...] = proj
    wide = proj.astype(F32)
    mixed = wide[chan : 2 * chan] * wide[2 * chan :]
    grad_conv = cot_ref[...].astype(F32) * wide[:chan]
    mixed = mixed.reshape(chan // 8, 8, width)
    grad_conv = grad_conv.reshape(chan // 8, 8, width)
    low = low_rows(mixed.shape)
    send_ref[:, 0] = jnp.where(low, mixed, pltpu.roll(grad_conv, HALF, 1)).astype(BF16)
    send_ref[:, 1] = jnp.where(low, pltpu.roll(mixed, HALF, 1), grad_conv).astype(BF16)


def matrices_kernel(group_ref, ids_ref, bank_ref, rhs_ref, bank_f32):
    stored = bank_ref.shape[1]
    bank_f32[...] = bank_ref[0].astype(F32)
    first = ids_ref[group_ref[0], 0]
    row = lax.broadcasted_iota(jnp.int32, (BLK, BLK), 0)
    col = lax.broadcasted_iota(jnp.int32, (BLK, BLK), 1)
    rhs_ref[stored // 2, :, BLK:] = jnp.zeros((2 * BLK, BLK), BF16)
    for f in range(stored + 1):
        taps = bank_f32[pl.ds(first if f == stored else f, 1), :]
        rows = jnp.broadcast_to(taps, (BLK, 2 * BLK))
        turned = pltpu.roll(rows, BLK, 1, stride=1, stride_axis=0)[:, :BLK]
        if f == stored:
            turned = jnp.where(col >= row, turned, 0.0)
        lanes = slice((f % 2) * BLK, (f % 2 + 1) * BLK)
        rhs_ref[f // 2, :BLK, lanes] = turned.astype(BF16)
        rhs_ref[f // 2, BLK:, lanes] = turned.T.astype(BF16)


def convolve_kernel(
    group_ref, lags_ref, ids_ref, x_ref, rhs_ref, out_ref, lhs, prod, res, *scratch
):
    conv_part(group_ref, lags_ref, ids_ref, x_ref, rhs_ref, out_ref, lhs, prod, res)
    filter_part(group_ref, lags_ref, ids_ref, x_ref, out_ref, *scratch)


def conv_part(group_ref, lags_ref, ids_ref, x_ref, rhs_ref, out_ref, lhs, prod, res):
    peers, _, tok = x_ref.shape
    per = tok // BLK
    blocks = peers * per
    pairs = rhs_ref.shape[0]
    stored = 2 * (pairs - 1)
    entries = lags_ref.shape[1]
    group = group_ref[0]
    low = low_rows((8, BLK))
    zero = jnp.zeros((8, BLK), F32)

    def tile(i):
        return x_ref[i // per, :, (i % per) * BLK : (i % per + 1) * BLK].astype(F32)

    for i in range(0, blocks, 2):
        left = [jnp.where(low, tile(i + j), zero) for j in (0, 1)]
        right = [jnp.where(low, zero, tile(blocks - 1 - i - j)) for j in (0, 1)]
        lhs[i * 8 : i * 8 + 16, :BLK] = jnp.concatenate(left, 0).astype(BF16)
        lhs[i * 8 : i * 8 + 16, BLK:] = jnp.concatenate(right, 0).astype(BF16)

    def product(pair, carry):
        both = jnp.dot(lhs[...], rhs_ref[pair], preferred_element_type=F32)
        for j in (0, 1):
            half = both[:, j * BLK : (j + 1) * BLK].reshape(blocks, 8, BLK)
            prod[2 * pair + j, blocks:] = half
            prod[2 * pair + j, :blocks] = jnp.zeros((blocks, 8, BLK), F32)
        return carry

    lax.fori_loop(0, pairs, product, 0)
    chunk = 24
    for start in range(0, blocks, chunk):

        def add(k, acc):
            return acc + prod[ids_ref[group, k], pl.ds(blocks + start - lags_ref[group, k], chunk)]

        acc = prod[stored, blocks + start : blocks + start + chunk]
        res[start : start + chunk] = lax.fori_loop(1, entries, add, acc)
    for i in range(blocks):
        both = jnp.where(low, res[i], res[blocks - 1 - i])
        out_ref[i // per, :, (i % per) * BLK : (i % per + 1) * BLK] = both.astype(BF16)


def filter_part(group_ref, lags_ref, ids_ref, x_ref, out_ref, padded, cots, turned, sums, folded):
    peers, _, tok = x_ref.shape
    per = tok // BLK
    blocks = peers * per
    entries = lags_ref.shape[1]
    stored = sums.shape[0]
    group = group_ref[0]
    low = low_rows((8, BLK))
    padded[:blocks] = jnp.zeros((blocks, 8, BLK), F32)
    for i in range(blocks):
        tile = x_ref[i // per, :, (i % per) * BLK : (i % per + 1) * BLK].astype(F32)
        padded[blocks + i] = jnp.where(low, tile, 0.0)
        cots[i] = jnp.where(low, pltpu.roll(tile, HALF, 0), 0.0)
    step = BLK // 8
    for j in range(blocks // step):
        rows = cots[j * step : (j + 1) * step].reshape(BLK, BLK)
        turned[:, j * BLK : (j + 1) * BLK] = rows.T.astype(BF16)
    sums[...] = jnp.zeros(sums.shape, F32)
    row = lax.broadcasted_iota(jnp.int32, (BLK, BLK), 0)
    col = lax.broadcasted_iota(jnp.int32, (BLK, BLK), 1)

    def pair(p, carry):
        k = 2 * p
        shifted = [padded[pl.ds(blocks - lags_ref[group, k + j], blocks)] for j in (0, 1)]
        shifted = [s.reshape(blocks * 8, BLK).astype(BF16) for s in shifted]
        both = jnp.dot(turned[...], jnp.concatenate(shifted, 1), preferred_element_type=F32)
        keep = (row >= col) | (k > 0)
        sums[ids_ref[group, k]] += jnp.where(keep, both[:, :BLK], 0.0)
        sums[ids_ref[group, k + 1]] += both[:, BLK:]
        return carry

    lax.fori_loop(0, entries // 2, pair, 0)
    for f in range(stored):
        mat = jnp.concatenate([jnp.zeros((BLK, BLK), F32), sums[f].T], 1)
        total = mat[:8]
        for q in range(1, BLK // 8):
            total += pltpu.roll(mat[8 * q : 8 * q + 8], 2 * BLK - 8 * q, 1)
        folded[f] = total
    total = folded[:, 0]
    for s in range(1, 8):
        total += pltpu.roll(folded[:, s], 2 * BLK - s, 1)
    high = total.astype(BF16).astype(F32)
    rest = total - high
    sub = lax.broadcasted_iota(jnp.int32, (8, BLK), 0)
    for p in range(peers):
        piece = jnp.zeros((8, BLK), F32)
        for r, part in enumerate((high[:, :BLK], high[:, BLK:], rest[:, :BLK], rest[:, BLK:])):
            piece = jnp.where(sub == r, part[p : p + 1], piece)
        out_ref[p, :, tok:] = piece.astype(BF16)


def weights_kernel(back_ref, proj_ref, cot_ref, tok_ref, gated_ref, out_ref, grads):
    chan, tok = cot_ref.shape

    @pl.when(pl.program_id(0) == 0)
    def _():
        even = back_ref[:, 0, :, :tok].astype(F32)
        odd = back_ref[:, 1, :, :tok].astype(F32)
        low = low_rows(even.shape)
        conv_out = jnp.where(low, even, pltpu.roll(odd, HALF, 1)).reshape(chan, tok)
        grad_mixed = jnp.where(low, pltpu.roll(even, HALF, 1), odd).reshape(chan, tok)
        gated_ref[...] = (proj_ref[:chan].astype(F32) * conv_out).astype(BF16)
        grads[:chan] = (cot_ref[...].astype(F32) * conv_out).astype(BF16)
        grads[chan : 2 * chan] = (grad_mixed * proj_ref[2 * chan :].astype(F32)).astype(BF16)
        grads[2 * chan :] = (grad_mixed * proj_ref[chan : 2 * chan].astype(F32)).astype(BF16)

    both = jnp.dot(grads[...], tok_ref[...], preferred_element_type=F32)
    share = out_ref.shape[2]
    for j in range(out_ref.shape[0]):
        out_ref[j] = both[:, j * share : (j + 1) * share].astype(out_ref.dtype)


def spread_kernel(back_ref, out_ref):
    both = jnp.sum(back_ref[...].astype(F32), axis=0)
    both += pltpu.roll(both, 6, 0)
    high = both.astype(BF16).astype(F32)
    sub = lax.broadcasted_iota(jnp.int32, both.shape, 0)
    piece = jnp.where(sub < 2, high, jnp.where(sub < 4, pltpu.roll(both - high, 2, 0), 0.0))
    out_ref[...] = jnp.broadcast_to(piece.astype(BF16)[None], out_ref.shape)


def append_kernel(got_ref, _, out_ref, held):
    groups = held.shape[0]
    both = got_ref[...].astype(F32)
    both += pltpu.roll(both, 6, 1)
    held[...] = jnp.sum(both.reshape(groups, -1, *both.shape[1:]), axis=1)
    rows = jnp.concatenate([held[:, 0], held[:, 1]], axis=1).astype(BF16)
    if out_ref.shape[1] > groups:
        rows = jnp.concatenate([rows, jnp.zeros((out_ref.shape[1] - groups, rows.shape[1]), BF16)], 0)
    out_ref[...] = jnp.broadcast_to(rows[None], out_ref.shape)


def finish_kernel(got_ref, w_ref, table_ref):
    rows = w_ref.shape[0]
    total = got_ref[0, :rows].astype(F32)
    for p in range(1, got_ref.shape[0]):
        total += got_ref[p, :rows].astype(F32)
    w_ref[...] = total
    for p in range(got_ref.shape[0]):
        table_ref[:, p] = got_ref[p, rows : rows + table_ref.shape[0]].astype(F32)


def whole(shape):
    return pl.BlockSpec(shape, lambda *_: (0,) * len(shape))


def params(mib):
    return pltpu.CompilerParams(vmem_limit_bytes=mib << 20)


def cost(flops, moved):
    return pl.CostEstimate(flops=flops, bytes_accessed=moved, transcendentals=0)


def local(tokens_in, w_in, filter_bank, lag_blocks, filter_ids, grad_out):
    chan, tok = grad_out.shape
    depth = tokens_in.shape[1]
    peers = lax.axis_size("ctx")
    blocks = tok * peers // BLK
    groups, stored, span = filter_bank.shape
    entries = lag_blocks.shape[1]
    share = depth // peers
    pairs = stored // 2 + 1
    group = (lax.axis_index("ch") // (lax.axis_size("ch") // groups)).astype(jnp.int32)[None]
    weights = jnp.transpose(w_in, (1, 2, 0)).reshape(3 * chan, depth)

    wide = 256
    proj, send = pl.pallas_call(
        project_kernel,
        grid=(tok // wide,),
        in_specs=[
            whole((3 * chan, depth)),
            pl.BlockSpec((wide, depth), lambda i: (i, 0)),
            pl.BlockSpec((chan, wide), lambda i: (0, i)),
        ],
        out_specs=[
            pl.BlockSpec((3 * chan, wide), lambda i: (0, i)),
            pl.BlockSpec((chan // 8, 2, 8, wide), lambda i: (0, 0, 0, i)),
        ],
        out_shape=[
            jax.ShapeDtypeStruct((3 * chan, tok), BF16),
            jax.ShapeDtypeStruct((chan // 8, 2, 8, tok), BF16),
        ],
        compiler_params=params(60),
        cost_estimate=cost(6 * chan * depth * tok, 2 * depth * (tok + 3 * chan)),
        name="project",
    )(weights, tokens_in, grad_out)
    rhs = pl.pallas_call(
        matrices_kernel,
        grid_spec=pltpu.PrefetchScalarGridSpec(
            num_scalar_prefetch=2,
            grid=(1,),
            in_specs=[pl.BlockSpec((1, stored, span), lambda i, g, ids: (g[0], 0, 0))],
            out_specs=whole((pairs, 2 * BLK, 2 * BLK)),
            scratch_shapes=[pltpu.VMEM((stored, span), F32)],
        ),
        out_shape=jax.ShapeDtypeStruct((pairs, 2 * BLK, 2 * BLK), BF16),
        compiler_params=params(60),
        cost_estimate=cost(pairs * 40 * BLK * BLK, pairs * 8 * BLK * BLK),
        name="matrices",
    )(group, filter_ids, filter_bank)
    seen = lax.all_to_all(send.reshape(peers, 8, tok), "ctx", 0, 0)
    back = pl.pallas_call(
        convolve_kernel,
        grid_spec=pltpu.PrefetchScalarGridSpec(
            num_scalar_prefetch=3,
            grid=(1,),
            in_specs=[whole((peers, 8, tok)), whole((pairs, 2 * BLK, 2 * BLK))],
            out_specs=whole((peers, 8, tok + BLK)),
            scratch_shapes=[
                pltpu.VMEM((blocks * 8, 2 * BLK), BF16),
                pltpu.VMEM((2 * pairs, 2 * blocks, 8, BLK), F32),
                pltpu.VMEM((blocks, 8, BLK), F32),
                pltpu.VMEM((2 * blocks, 8, BLK), F32),
                pltpu.VMEM((blocks, 8, BLK), F32),
                pltpu.VMEM((BLK, blocks * 8), BF16),
                pltpu.VMEM((stored, BLK, BLK), F32),
                pltpu.VMEM((stored, 8, span), F32),
            ],
        ),
        out_shape=jax.ShapeDtypeStruct((peers, 8, tok + BLK), BF16),
        compiler_params=params(60),
        cost_estimate=cost(pairs * 16 * blocks * 8 * BLK * BLK, peers * 32 * tok),
        name="convolve",
    )(group, lag_blocks, filter_ids, seen, rhs)
    got = lax.all_to_all(back, "ctx", 0, 0)
    lines = lax.axis_size("ch")
    piece = pl.pallas_call(
        spread_kernel,
        grid=(1,),
        in_specs=[pl.BlockSpec((peers, 8, BLK), lambda i: (0, 0, tok // BLK))],
        out_specs=whole((lines, 8, BLK)),
        out_shape=jax.ShapeDtypeStruct((lines, 8, BLK), BF16),
        compiler_params=params(60),
        name="spread",
    )(got)
    tables = lax.all_to_all(piece, "ch", 0, 0)
    chunk = 2
    rows = 3 * chan
    lines_in = -(-groups // 8) * 8
    gated, partial = pl.pallas_call(
        weights_kernel,
        grid=(peers // chunk,),
        in_specs=[
            whole((chan // 8, 2, 8, tok + BLK)),
            whole((rows, tok)),
            whole((chan, tok)),
            pl.BlockSpec((tok, chunk * share), lambda i: (0, i)),
        ],
        out_specs=[
            whole((chan, tok)),
            pl.BlockSpec((chunk, rows, share), lambda i: (i, 0, 0)),
        ],
        out_shape=[
            jax.ShapeDtypeStruct((chan, tok), BF16),
            jax.ShapeDtypeStruct((peers, rows + lines_in, share), BF16),
        ],
        scratch_shapes=[pltpu.VMEM((rows, tok), BF16)],
        compiler_params=params(60),
        cost_estimate=cost(6 * chan * depth * tok, 2 * depth * (tok + 6 * chan)),
        name="weights",
    )(got.reshape(chan // 8, 2, 8, tok + BLK), proj, grad_out, tokens_in)
    partial = pl.pallas_call(
        append_kernel,
        grid=(1,),
        in_specs=[whole((lines, 8, BLK)), pl.BlockSpec(memory_space=pl.ANY)],
        out_specs=pl.BlockSpec((peers, lines_in, share), lambda i: (0, rows // lines_in, 0)),
        out_shape=jax.ShapeDtypeStruct(partial.shape, BF16),
        scratch_shapes=[pltpu.VMEM((groups, 8, BLK), F32)],
        input_output_aliases={1: 0},
        compiler_params=params(60),
        name="append",
    )(tables, partial)
    parts = lax.all_to_all(partial, "ctx", 0, 0)
    w_grad, filter_grad = pl.pallas_call(
        finish_kernel,
        grid=(1,),
        in_specs=[whole(parts.shape)],
        out_specs=[whole((rows, share)), whole((groups, peers, share))],
        out_shape=[
            jax.ShapeDtypeStruct((rows, share), F32),
            jax.ShapeDtypeStruct((groups, peers, share), F32),
        ],
        compiler_params=params(60),
        name="finish",
    )(parts)
    w_grad = jnp.transpose(w_grad.reshape(3, chan, share), (2, 0, 1))
    return gated, w_grad, filter_grad


def solution(mesh):
    placed = (P("ctx", None), P(None, None, "ch"), P(), P(), P(), P("ch", "ctx"))
    return jax.shard_map(
        local,
        mesh=mesh,
        in_specs=placed,
        out_specs=(P("ch", "ctx"), P("ctx", None, "ch"), P()),
        check_vma=False,
    )
```

```python
import jax
import jax.numpy as jnp
from jax import lax
from jax.experimental import pallas as pl
from jax.experimental.pallas import tpu as pltpu
from jax.sharding import PartitionSpec as P

BLK = 128
CHUNK = 24
HALF = 4
BF16, F32 = jnp.bfloat16, jnp.float32


def low_rows(shape):
    return lax.broadcasted_iota(jnp.int32, shape, len(shape) - 2) < HALF


def project_kernel(w_ref, tok_ref, cot_ref, proj_ref, send_ref, acc):
    chan, tok = cot_ref.shape
    step = pl.program_id(0)
    part = lax.dot_general(
        w_ref[...], tok_ref[...], (((1,), (1,)), ((), ())), preferred_element_type=F32
    )

    @pl.when(step == 0)
    def _():
        acc[...] = part

    @pl.when(step > 0)
    def _():
        acc[...] += part

    @pl.when(step == pl.num_programs(0) - 1)
    def _():
        proj = acc[...].astype(BF16)
        proj_ref[...] = proj
        wide = proj.astype(F32)
        mixed = wide[chan : 2 * chan] * wide[2 * chan :]
        grad_conv = cot_ref[...].astype(F32) * wide[:chan]
        mixed = mixed.reshape(chan // 8, 8, tok)
        grad_conv = grad_conv.reshape(chan // 8, 8, tok)
        low = low_rows(mixed.shape)
        send_ref[:, 0] = jnp.where(low, mixed, pltpu.roll(grad_conv, HALF, 1)).astype(BF16)
        send_ref[:, 1] = jnp.where(low, pltpu.roll(mixed, HALF, 1), grad_conv).astype(BF16)


def matrices_kernel(group_ref, ids_ref, bank_ref, rhs_ref, bank_f32):
    stored = bank_ref.shape[1]
    bank_f32[...] = bank_ref[0].astype(F32)
    first = ids_ref[group_ref[0], 0]
    row = lax.broadcasted_iota(jnp.int32, (BLK, BLK), 0)
    col = lax.broadcasted_iota(jnp.int32, (BLK, BLK), 1)
    rhs_ref[stored // 2, :, BLK:] = jnp.zeros((2 * BLK, BLK), BF16)
    for f in range(stored + 1):
        taps = bank_f32[pl.ds(first if f == stored else f, 1), :]
        rows = jnp.broadcast_to(taps, (BLK, 2 * BLK))
        turned = pltpu.roll(rows, BLK, 1, stride=1, stride_axis=0)[:, :BLK]
        if f == stored:
            turned = jnp.where(col >= row, turned, 0.0)
        lanes = slice((f % 2) * BLK, (f % 2 + 1) * BLK)
        rhs_ref[f // 2, :BLK, lanes] = turned.astype(BF16)
        rhs_ref[f // 2, BLK:, lanes] = turned.T.astype(BF16)


def convolve_kernel(
    group_ref, lags_ref, ids_ref, x_ref, rhs_ref, out_ref, lhs, prod, res, *scratch
):
    conv_part(group_ref, lags_ref, ids_ref, x_ref, rhs_ref, out_ref, lhs, prod, res)
    filter_part(group_ref, lags_ref, ids_ref, x_ref, out_ref, *scratch)


def conv_part(group_ref, lags_ref, ids_ref, x_ref, rhs_ref, out_ref, lhs, prod, res):
    peers, _, tok = x_ref.shape
    per = tok // BLK
    blocks = peers * per
    pairs = rhs_ref.shape[0]
    stored = 2 * (pairs - 1)
    entries = lags_ref.shape[1]
    group = group_ref[0]
    low = low_rows((8, BLK))
    zero = jnp.zeros((8, BLK), F32)

    def tile(i):
        return x_ref[i // per, :, (i % per) * BLK : (i % per + 1) * BLK].astype(F32)

    for i in range(0, blocks, 2):
        left = [jnp.where(low, tile(i + j), zero) for j in (0, 1)]
        right = [jnp.where(low, zero, tile(blocks - 1 - i - j)) for j in (0, 1)]
        lhs[i * 8 : i * 8 + 16, :BLK] = jnp.concatenate(left, 0).astype(BF16)
        lhs[i * 8 : i * 8 + 16, BLK:] = jnp.concatenate(right, 0).astype(BF16)

    def product(pair, carry):
        both = jnp.dot(lhs[...], rhs_ref[pair], preferred_element_type=F32)
        for j in (0, 1):
            half = both[:, j * BLK : (j + 1) * BLK].reshape(blocks, 8, BLK)
            prod[2 * pair + j, CHUNK:] = half
            prod[2 * pair + j, :CHUNK] = jnp.zeros((CHUNK, 8, BLK), F32)
        return carry

    lax.fori_loop(0, pairs, product, 0, unroll=True)
    for start in range(0, blocks, CHUNK):

        def add(k, acc):
            first = jnp.maximum(CHUNK + start - lags_ref[group, k], 0)
            return acc + prod[ids_ref[group, k], pl.ds(first, CHUNK)]

        acc = prod[stored, CHUNK + start : 2 * CHUNK + start]
        res[start : start + CHUNK] = lax.fori_loop(1, entries, add, acc, unroll=True)
    for i in range(blocks):
        both = jnp.where(low, res[i], res[blocks - 1 - i])
        out_ref[i // per, :, (i % per) * BLK : (i % per + 1) * BLK] = both.astype(BF16)


def filter_part(group_ref, lags_ref, ids_ref, x_ref, out_ref, padded, cots, turned, sums, folded):
    peers, _, tok = x_ref.shape
    per = tok // BLK
    blocks = peers * per
    entries = lags_ref.shape[1]
    stored = sums.shape[0]
    group = group_ref[0]
    low = low_rows((8, BLK))
    padded[:blocks] = jnp.zeros((blocks, 8, BLK), F32)
    for i in range(blocks):
        tile = x_ref[i // per, :, (i % per) * BLK : (i % per + 1) * BLK].astype(F32)
        other = pltpu.roll(tile, HALF, 0)
        padded[blocks + i] = jnp.where(low, tile, other)
        cots[0, i] = jnp.where(low, other, 0.0)
        cots[1, i] = jnp.where(low, 0.0, tile)
    step = BLK // 8
    for h in (0, 1):
        for j in range(blocks // step):
            rows = cots[h, j * step : (j + 1) * step].reshape(BLK, BLK)
            turned[h * BLK : (h + 1) * BLK, j * BLK : (j + 1) * BLK] = rows.T.astype(BF16)
    sums[...] = jnp.zeros(sums.shape, F32)
    row = lax.broadcasted_iota(jnp.int32, (BLK, BLK), 0)
    col = lax.broadcasted_iota(jnp.int32, (BLK, BLK), 1)
    low_all = low_rows((blocks, 8, BLK))

    def four(p, carry):
        sides = []
        for j in (0, 2):
            top, bottom = (padded[pl.ds(blocks - lags_ref[group, 4 * p + j + h], blocks)] for h in (0, 1))
            sides.append(jnp.where(low_all, top, bottom).reshape(blocks * 8, BLK).astype(BF16))
        both = jnp.dot(turned[...], jnp.concatenate(sides, 1), preferred_element_type=F32)
        keep = (row >= col) | (p > 0)
        for j in range(4):
            part = both[(j % 2) * BLK : (j % 2 + 1) * BLK, (j // 2) * BLK : (j // 2 + 1) * BLK]
            sums[ids_ref[group, 4 * p + j]] += jnp.where(keep, part, 0.0) if j == 0 else part
        return carry

    lax.fori_loop(0, entries // 4, four, 0, unroll=True)
    for f in range(stored):
        mat = jnp.concatenate([jnp.zeros((BLK, BLK), F32), sums[f].T], 1)
        total = mat[:8]
        for q in range(1, BLK // 8):
            total += pltpu.roll(mat[8 * q : 8 * q + 8], 2 * BLK - 8 * q, 1)
        folded[f] = total
    total = folded[:, 0]
    for s in range(1, 8):
        total += pltpu.roll(folded[:, s], 2 * BLK - s, 1)
    high = total.astype(BF16).astype(F32)
    rest = total - high
    sub = lax.broadcasted_iota(jnp.int32, (8, BLK), 0)
    for p in range(peers):
        piece = jnp.zeros((8, BLK), F32)
        for r, part in enumerate((high[:, :BLK], high[:, BLK:], rest[:, :BLK], rest[:, BLK:])):
            piece = jnp.where(sub == r, part[p : p + 1], piece)
        out_ref[p, :, tok:] = piece.astype(BF16)


def weights_kernel(back_ref, proj_ref, cot_ref, tok_ref, gated_ref, out_ref, grads):
    chan, tok = cot_ref.shape

    @pl.when(pl.program_id(0) == 0)
    def _():
        even = back_ref[:, 0, :, :tok].astype(F32)
        odd = back_ref[:, 1, :, :tok].astype(F32)
        low = low_rows(even.shape)
        conv_out = jnp.where(low, even, pltpu.roll(odd, HALF, 1)).reshape(chan, tok)
        grad_mixed = jnp.where(low, pltpu.roll(even, HALF, 1), odd).reshape(chan, tok)
        gated_ref[...] = (proj_ref[:chan].astype(F32) * conv_out).astype(BF16)
        grads[:chan] = (cot_ref[...].astype(F32) * conv_out).astype(BF16)
        grads[chan : 2 * chan] = (grad_mixed * proj_ref[2 * chan :].astype(F32)).astype(BF16)
        grads[2 * chan :] = (grad_mixed * proj_ref[chan : 2 * chan].astype(F32)).astype(BF16)

    both = jnp.dot(grads[...], tok_ref[...], preferred_element_type=F32)
    share = out_ref.shape[2]
    for j in range(out_ref.shape[0]):
        out_ref[j] = both[:, j * share : (j + 1) * share].astype(out_ref.dtype)


def spread_kernel(back_ref, out_ref):
    both = jnp.sum(back_ref[...].astype(F32), axis=0)
    both += pltpu.roll(both, 6, 0)
    high = both.astype(BF16).astype(F32)
    sub = lax.broadcasted_iota(jnp.int32, both.shape, 0)
    piece = jnp.where(sub < 2, high, jnp.where(sub < 4, pltpu.roll(both - high, 2, 0), 0.0))
    out_ref[...] = jnp.broadcast_to(piece.astype(BF16)[None], out_ref.shape)


def append_kernel(got_ref, _, out_ref, held):
    groups = held.shape[0]
    both = got_ref[...].astype(F32)
    both += pltpu.roll(both, 6, 1)
    held[...] = jnp.sum(both.reshape(groups, -1, *both.shape[1:]), axis=1)
    rows = jnp.concatenate([held[:, 0], held[:, 1]], axis=1).astype(BF16)
    if out_ref.shape[1] > groups:
        rows = jnp.concatenate([rows, jnp.zeros((out_ref.shape[1] - groups, rows.shape[1]), BF16)], 0)
    out_ref[...] = jnp.broadcast_to(rows[None], out_ref.shape)


def finish_kernel(got_ref, w_ref, table_ref):
    rows = w_ref.shape[0]
    total = got_ref[0, :rows].astype(F32)
    for p in range(1, got_ref.shape[0]):
        total += got_ref[p, :rows].astype(F32)
    w_ref[...] = total
    for p in range(got_ref.shape[0]):
        table_ref[:, p] = got_ref[p, rows : rows + table_ref.shape[0]].astype(F32)


def whole(shape):
    return pl.BlockSpec(shape, lambda *_: (0,) * len(shape))


def params(mib):
    return pltpu.CompilerParams(vmem_limit_bytes=mib << 20)


def cost(flops, moved):
    return pl.CostEstimate(flops=flops, bytes_accessed=moved, transcendentals=0)


def local(tokens_in, w_in, filter_bank, lag_blocks, filter_ids, grad_out):
    chan, tok = grad_out.shape
    depth = tokens_in.shape[1]
    peers = lax.axis_size("ctx")
    blocks = tok * peers // BLK
    groups, stored, span = filter_bank.shape
    entries = lag_blocks.shape[1]
    share = depth // peers
    pairs = stored // 2 + 1
    group = (lax.axis_index("ch") // (lax.axis_size("ch") // groups)).astype(jnp.int32)[None]
    weights = jnp.transpose(w_in, (1, 2, 0)).reshape(3 * chan, depth)
    weights = pltpu.with_memory_space_constraint(weights, pltpu.HBM)
    tokens_in = pltpu.with_memory_space_constraint(tokens_in, pltpu.HBM)
    grad_out = pltpu.with_memory_space_constraint(grad_out, pltpu.HBM)

    deep = depth // 4
    proj, send = pl.pallas_call(
        project_kernel,
        grid=(depth // deep,),
        in_specs=[
            pl.BlockSpec((3 * chan, deep), lambda i: (0, i)),
            pl.BlockSpec((tok, deep), lambda i: (0, i)),
            whole((chan, tok)),
        ],
        out_specs=[whole((3 * chan, tok)), whole((chan // 8, 2, 8, tok))],
        scratch_shapes=[pltpu.VMEM((3 * chan, tok), F32)],
        out_shape=[
            jax.ShapeDtypeStruct((3 * chan, tok), BF16),
            jax.ShapeDtypeStruct((chan // 8, 2, 8, tok), BF16),
        ],
        compiler_params=params(20),
        cost_estimate=cost(6 * chan * depth * tok, 2 * depth * (tok + 3 * chan)),
        name="project",
    )(weights, tokens_in, grad_out)
    rhs = pl.pallas_call(
        matrices_kernel,
        grid_spec=pltpu.PrefetchScalarGridSpec(
            num_scalar_prefetch=2,
            grid=(1,),
            in_specs=[pl.BlockSpec((1, stored, span), lambda i, g, ids: (g[0], 0, 0))],
            out_specs=whole((pairs, 2 * BLK, 2 * BLK)),
            scratch_shapes=[pltpu.VMEM((stored, span), F32)],
        ),
        out_shape=jax.ShapeDtypeStruct((pairs, 2 * BLK, 2 * BLK), BF16),
        compiler_params=params(8),
        cost_estimate=cost(pairs * 40 * BLK * BLK, pairs * 8 * BLK * BLK),
        name="matrices",
    )(group, filter_ids, filter_bank)
    seen = lax.all_to_all(send.reshape(peers, 8, tok), "ctx", 0, 0)
    back = pl.pallas_call(
        convolve_kernel,
        grid_spec=pltpu.PrefetchScalarGridSpec(
            num_scalar_prefetch=3,
            grid=(1,),
            in_specs=[whole((peers, 8, tok)), whole((pairs, 2 * BLK, 2 * BLK))],
            out_specs=whole((peers, 8, tok + BLK)),
            scratch_shapes=[
                pltpu.VMEM((blocks * 8, 2 * BLK), BF16),
                pltpu.VMEM((2 * pairs, blocks + CHUNK, 8, BLK), F32),
                pltpu.VMEM((blocks, 8, BLK), F32),
                pltpu.VMEM((2 * blocks, 8, BLK), F32),
                pltpu.VMEM((2, blocks, 8, BLK), F32),
                pltpu.VMEM((2 * BLK, blocks * 8), BF16),
                pltpu.VMEM((stored, BLK, BLK), F32),
                pltpu.VMEM((stored, 8, span), F32),
            ],
        ),
        out_shape=jax.ShapeDtypeStruct((peers, 8, tok + BLK), BF16),
        compiler_params=params(24),
        cost_estimate=cost(pairs * 16 * blocks * 8 * BLK * BLK, peers * 32 * tok),
        name="convolve",
    )(group, lag_blocks, filter_ids, seen, rhs)
    got = lax.all_to_all(back, "ctx", 0, 0)
    lines = lax.axis_size("ch")
    piece = pl.pallas_call(
        spread_kernel,
        grid=(1,),
        in_specs=[pl.BlockSpec((peers, 8, BLK), lambda i: (0, 0, tok // BLK))],
        out_specs=whole((lines, 8, BLK)),
        out_shape=jax.ShapeDtypeStruct((lines, 8, BLK), BF16),
        compiler_params=params(4),
        name="spread",
    )(got)
    tables = lax.all_to_all(piece, "ch", 0, 0)
    chunk = 2
    rows = 3 * chan
    lines_in = -(-groups // 8) * 8
    gated, partial = pl.pallas_call(
        weights_kernel,
        grid=(peers // chunk,),
        in_specs=[
            whole((chan // 8, 2, 8, tok + BLK)),
            whole((rows, tok)),
            whole((chan, tok)),
            pl.BlockSpec((tok, chunk * share), lambda i: (0, i)),
        ],
        out_specs=[
            whole((chan, tok)),
            pl.BlockSpec((chunk, rows, share), lambda i: (i, 0, 0)),
        ],
        out_shape=[
            jax.ShapeDtypeStruct((chan, tok), BF16),
            jax.ShapeDtypeStruct((peers, rows + lines_in, share), BF16),
        ],
        scratch_shapes=[pltpu.VMEM((rows, tok), BF16)],
        compiler_params=params(20),
        cost_estimate=cost(6 * chan * depth * tok, 2 * depth * (tok + 6 * chan)),
        name="weights",
    )(got.reshape(chan // 8, 2, 8, tok + BLK), proj, grad_out, tokens_in)
    partial = pl.pallas_call(
        append_kernel,
        grid=(1,),
        in_specs=[whole((lines, 8, BLK)), pl.BlockSpec(memory_space=pl.ANY)],
        out_specs=pl.BlockSpec((peers, lines_in, share), lambda i: (0, rows // lines_in, 0)),
        out_shape=jax.ShapeDtypeStruct(partial.shape, BF16),
        scratch_shapes=[pltpu.VMEM((groups, 8, BLK), F32)],
        input_output_aliases={1: 0},
        compiler_params=params(8),
        name="append",
    )(tables, partial)
    parts = lax.all_to_all(partial, "ctx", 0, 0)
    w_grad, filter_grad = pl.pallas_call(
        finish_kernel,
        grid=(1,),
        in_specs=[whole(parts.shape)],
        out_specs=[whole((rows, share)), whole((groups, peers, share))],
        out_shape=[
            jax.ShapeDtypeStruct((rows, share), F32),
            jax.ShapeDtypeStruct((groups, peers, share), F32),
        ],
        compiler_params=params(10),
        name="finish",
    )(parts)
    w_grad = jnp.transpose(w_grad.reshape(3, chan, share), (2, 0, 1))
    return gated, w_grad, filter_grad


def solution(mesh):
    placed = (P("ctx", None), P(None, None, "ch"), P(), P(), P(), P("ch", "ctx"))
    return jax.shard_map(
        local,
        mesh=mesh,
        in_specs=placed,
        out_specs=(P("ch", "ctx"), P("ctx", None, "ch"), P()),
        check_vma=False,
    )
```

```python
import jax
import jax.numpy as jnp
from jax import lax
from jax.experimental import pallas as pl
from jax.experimental.pallas import tpu as pltpu
from jax.sharding import PartitionSpec as P

BLK = 128
CHUNK = 24
LINE = 4
HALF = 4
BF16, F32 = jnp.bfloat16, jnp.float32


def low_rows(shape):
    return lax.broadcasted_iota(jnp.int32, shape, len(shape) - 2) < HALF


def project_kernel(w_ref, tok_ref, cot_ref, proj_ref, send_ref, acc):
    chan, tok = cot_ref.shape
    step = pl.program_id(0)
    part = lax.dot_general(
        w_ref[...], tok_ref[...], (((1,), (1,)), ((), ())), preferred_element_type=F32
    )

    @pl.when(step == 0)
    def _():
        acc[...] = part

    @pl.when(step > 0)
    def _():
        acc[...] += part

    @pl.when(step == pl.num_programs(0) - 1)
    def _():
        proj = acc[...].astype(BF16)
        proj_ref[...] = proj
        wide = proj.astype(F32)
        mixed = wide[chan : 2 * chan] * wide[2 * chan :]
        grad_conv = cot_ref[...].astype(F32) * wide[:chan]
        mixed = mixed.reshape(chan // 8, 8, tok)
        grad_conv = grad_conv.reshape(chan // 8, 8, tok)
        low = low_rows(mixed.shape)
        send_ref[:, 0] = jnp.where(low, mixed, pltpu.roll(grad_conv, HALF, 1)).astype(BF16)
        send_ref[:, 1] = jnp.where(low, pltpu.roll(mixed, HALF, 1), grad_conv).astype(BF16)


def matrices_kernel(group_ref, ids_ref, bank_ref, rhs_ref, bank_f32):
    stored = bank_ref.shape[1]
    bank_f32[...] = bank_ref[0].astype(F32)
    first = ids_ref[group_ref[0], 0]
    row = lax.broadcasted_iota(jnp.int32, (BLK, BLK), 0)
    col = lax.broadcasted_iota(jnp.int32, (BLK, BLK), 1)
    rhs_ref[stored // 2, :, BLK:] = jnp.zeros((2 * BLK, BLK), BF16)
    for f in range(stored + 1):
        taps = bank_f32[pl.ds(first if f == stored else f, 1), :]
        rows = jnp.broadcast_to(taps, (BLK, 2 * BLK))
        turned = pltpu.roll(rows, BLK, 1, stride=1, stride_axis=0)[:, :BLK]
        if f == stored:
            turned = jnp.where(col >= row, turned, 0.0)
        lanes = slice((f % 2) * BLK, (f % 2 + 1) * BLK)
        rhs_ref[f // 2, :BLK, lanes] = turned.astype(BF16)
        rhs_ref[f // 2, BLK:, lanes] = turned.T.astype(BF16)


def convolve_kernel(
    group_ref, lags_ref, ids_ref, x_ref, rhs_ref, out_ref, lhs, prod, res, *scratch
):
    conv_part(group_ref, lags_ref, ids_ref, x_ref, rhs_ref, out_ref, lhs, prod, res)
    filter_part(group_ref, lags_ref, ids_ref, x_ref, out_ref, *scratch)


def conv_part(group_ref, lags_ref, ids_ref, x_ref, rhs_ref, out_ref, lhs, prod, res):
    peers, _, tok = x_ref.shape
    per = tok // BLK
    blocks = peers * per
    pairs = rhs_ref.shape[0]
    stored = 2 * (pairs - 1)
    entries = lags_ref.shape[1]
    group = group_ref[0]
    low = low_rows((8, BLK))
    zero = jnp.zeros((8, BLK), F32)

    def tile(i):
        return x_ref[i // per, :, (i % per) * BLK : (i % per + 1) * BLK].astype(F32)

    for i in range(0, blocks, 2):
        left = [jnp.where(low, tile(i + j), zero) for j in (0, 1)]
        right = [jnp.where(low, zero, tile(blocks - 1 - i - j)) for j in (0, 1)]
        lhs[i * 8 : i * 8 + 16, :BLK] = jnp.concatenate(left, 0).astype(BF16)
        lhs[i * 8 : i * 8 + 16, BLK:] = jnp.concatenate(right, 0).astype(BF16)

    def product(pair, carry):
        both = jnp.dot(lhs[...], rhs_ref[pair], preferred_element_type=F32)
        for j in (0, 1):
            half = both[:, j * BLK : (j + 1) * BLK].reshape(blocks, 8, BLK)
            prod[2 * pair + j, CHUNK:] = half
            prod[2 * pair + j, :CHUNK] = jnp.zeros((CHUNK, 8, BLK), F32)
        return carry

    lax.fori_loop(0, pairs, product, 0, unroll=True)
    for start in range(0, blocks, CHUNK):

        def add(k, acc):
            first = jnp.maximum(CHUNK + start - lags_ref[group, k], 0)
            return acc + prod[ids_ref[group, k], pl.ds(first, CHUNK)]

        acc = prod[stored, CHUNK + start : 2 * CHUNK + start]
        res[start : start + CHUNK] = lax.fori_loop(1, entries, add, acc, unroll=True)
    for i in range(blocks):
        both = jnp.where(low, res[i], res[blocks - 1 - i])
        out_ref[i // per, :, (i % per) * BLK : (i % per + 1) * BLK] = both.astype(BF16)


def filter_part(group_ref, lags_ref, ids_ref, x_ref, out_ref, padded, cots, turned, sums, folded):
    peers, _, tok = x_ref.shape
    per = tok // BLK
    blocks = peers * per
    entries = lags_ref.shape[1]
    stored = sums.shape[0]
    group = group_ref[0]
    low = low_rows((8, BLK))
    padded[:blocks] = jnp.zeros((blocks, 8, BLK), F32)
    for i in range(blocks):
        tile = x_ref[i // per, :, (i % per) * BLK : (i % per + 1) * BLK].astype(F32)
        other = pltpu.roll(tile, HALF, 0)
        padded[blocks + i] = jnp.where(low, tile, other)
        cots[0, i] = jnp.where(low, other, 0.0)
        cots[1, i] = jnp.where(low, 0.0, tile)
    step = BLK // 8
    for h in (0, 1):
        for j in range(blocks // step):
            rows = cots[h, j * step : (j + 1) * step].reshape(BLK, BLK)
            turned[h * BLK : (h + 1) * BLK, j * BLK : (j + 1) * BLK] = rows.T.astype(BF16)
    sums[...] = jnp.zeros(sums.shape, F32)
    row = lax.broadcasted_iota(jnp.int32, (BLK, BLK), 0)
    col = lax.broadcasted_iota(jnp.int32, (BLK, BLK), 1)
    low_all = low_rows((blocks, 8, BLK))

    def four(p, carry):
        sides = []
        for j in (0, 2):
            top, bottom = (padded[pl.ds(blocks - lags_ref[group, 4 * p + j + h], blocks)] for h in (0, 1))
            sides.append(jnp.where(low_all, top, bottom).reshape(blocks * 8, BLK).astype(BF16))
        both = jnp.dot(turned[...], jnp.concatenate(sides, 1), preferred_element_type=F32)
        keep = (row >= col) | (p > 0)
        for j in range(4):
            part = both[(j % 2) * BLK : (j % 2 + 1) * BLK, (j // 2) * BLK : (j // 2 + 1) * BLK]
            sums[ids_ref[group, 4 * p + j]] += jnp.where(keep, part, 0.0) if j == 0 else part
        return carry

    lax.fori_loop(0, entries // 4, four, 0, unroll=True)
    for f in range(stored):
        mat = jnp.concatenate([jnp.zeros((BLK, BLK), F32), sums[f].T], 1)
        total = mat[:8]
        for q in range(1, BLK // 8):
            total += pltpu.roll(mat[8 * q : 8 * q + 8], 2 * BLK - 8 * q, 1)
        folded[f] = total
    total = folded[:, 0]
    for s in range(1, 8):
        total += pltpu.roll(folded[:, s], 2 * BLK - s, 1)
    sub = lax.broadcasted_iota(jnp.int32, (8, BLK), 0)
    per_line = stored // LINE
    for x in range(LINE):
        piece = jnp.zeros((8, BLK), F32)
        for r in range(2 * per_line):
            f = (r // 2) * LINE + x
            piece = jnp.where(sub == r, total[f : f + 1, (r % 2) * BLK : (r % 2 + 1) * BLK], piece)
        for p in range(x, peers, LINE):
            out_ref[p, :, tok:] = piece.astype(BF16)


def weights_kernel(back_ref, proj_ref, cot_ref, tok_ref, gated_ref, out_ref, grads):
    chan, tok = cot_ref.shape

    @pl.when(pl.program_id(0) == 0)
    def _():
        even = back_ref[:, 0, :, :tok].astype(F32)
        odd = back_ref[:, 1, :, :tok].astype(F32)
        low = low_rows(even.shape)
        conv_out = jnp.where(low, even, pltpu.roll(odd, HALF, 1)).reshape(chan, tok)
        grad_mixed = jnp.where(low, pltpu.roll(even, HALF, 1), odd).reshape(chan, tok)
        gated_ref[...] = (proj_ref[:chan].astype(F32) * conv_out).astype(BF16)
        grads[:chan] = (cot_ref[...].astype(F32) * conv_out).astype(BF16)
        grads[chan : 2 * chan] = (grad_mixed * proj_ref[2 * chan :].astype(F32)).astype(BF16)
        grads[2 * chan :] = (grad_mixed * proj_ref[chan : 2 * chan].astype(F32)).astype(BF16)

    both = jnp.dot(grads[...], tok_ref[...], preferred_element_type=F32)
    share = out_ref.shape[2]
    for j in range(out_ref.shape[0]):
        out_ref[j] = both[:, j * share : (j + 1) * share].astype(out_ref.dtype)


def spread_kernel(back_ref, out_ref):
    both = jnp.sum(back_ref[...].astype(F32), axis=0)
    out_ref[...] = jnp.broadcast_to(both.astype(BF16)[None], out_ref.shape)


def append_kernel(got_ref, _, out_ref, held):
    groups = held.shape[0]
    both = got_ref[...].astype(F32)
    held[...] = jnp.sum(both.reshape(groups, -1, *both.shape[1:]), axis=1)
    lines_in = out_ref.shape[1] // (held.shape[1] // 2)
    for j in range(held.shape[1] // 2):
        rows = jnp.concatenate([held[:, 2 * j], held[:, 2 * j + 1]], axis=1).astype(BF16)
        rows = jnp.broadcast_to(rows[None], (out_ref.shape[0], *rows.shape))
        out_ref[:, j * lines_in : j * lines_in + groups] = rows


def fold_kernel(got_ref, w_ref, table_ref):
    lines, rows = w_ref.shape[:2]
    for y in range(lines):
        total = got_ref[0, y * rows : (y + 1) * rows].astype(F32)
        for x in range(1, got_ref.shape[0]):
            total += got_ref[x, y * rows : (y + 1) * rows].astype(F32)
        w_ref[y] = total.astype(BF16)
    groups, stored = table_ref.shape[:2]
    per_line = stored // LINE
    lines_in = (got_ref.shape[1] - lines * rows) // per_line
    for f in range(stored):
        start = lines * rows + (f // LINE) * lines_in
        table_ref[:, f] = got_ref[f % LINE, start : start + groups].astype(F32)


def whole(shape):
    return pl.BlockSpec(shape, lambda *_: (0,) * len(shape))


def params(mib):
    return pltpu.CompilerParams(vmem_limit_bytes=mib << 20)


def cost(flops, moved):
    return pl.CostEstimate(flops=flops, bytes_accessed=moved, transcendentals=0)


def local(tokens_in, w_in, filter_bank, lag_blocks, filter_ids, grad_out):
    chan, tok = grad_out.shape
    depth = tokens_in.shape[1]
    peers = lax.axis_size("ctx")
    blocks = tok * peers // BLK
    groups, stored, span = filter_bank.shape
    entries = lag_blocks.shape[1]
    share = depth // peers
    pairs = stored // 2 + 1
    group = (lax.axis_index("ch") // (lax.axis_size("ch") // groups)).astype(jnp.int32)[None]
    weights = jnp.transpose(w_in, (1, 2, 0)).reshape(3 * chan, depth)
    weights = pltpu.with_memory_space_constraint(weights, pltpu.HBM)
    tokens_in = pltpu.with_memory_space_constraint(tokens_in, pltpu.HBM)
    grad_out = pltpu.with_memory_space_constraint(grad_out, pltpu.HBM)

    deep = depth // 4
    proj, send = pl.pallas_call(
        project_kernel,
        grid=(depth // deep,),
        in_specs=[
            pl.BlockSpec((3 * chan, deep), lambda i: (0, i)),
            pl.BlockSpec((tok, deep), lambda i: (0, i)),
            whole((chan, tok)),
        ],
        out_specs=[whole((3 * chan, tok)), whole((chan // 8, 2, 8, tok))],
        scratch_shapes=[pltpu.VMEM((3 * chan, tok), F32)],
        out_shape=[
            jax.ShapeDtypeStruct((3 * chan, tok), BF16),
            jax.ShapeDtypeStruct((chan // 8, 2, 8, tok), BF16),
        ],
        compiler_params=params(20),
        cost_estimate=cost(6 * chan * depth * tok, 2 * depth * (tok + 3 * chan)),
        name="project",
    )(weights, tokens_in, grad_out)
    rhs = pl.pallas_call(
        matrices_kernel,
        grid_spec=pltpu.PrefetchScalarGridSpec(
            num_scalar_prefetch=2,
            grid=(1,),
            in_specs=[pl.BlockSpec((1, stored, span), lambda i, g, ids: (g[0], 0, 0))],
            out_specs=whole((pairs, 2 * BLK, 2 * BLK)),
            scratch_shapes=[pltpu.VMEM((stored, span), F32)],
        ),
        out_shape=jax.ShapeDtypeStruct((pairs, 2 * BLK, 2 * BLK), BF16),
        compiler_params=params(8),
        cost_estimate=cost(pairs * 40 * BLK * BLK, pairs * 8 * BLK * BLK),
        name="matrices",
    )(group, filter_ids, filter_bank)
    seen = lax.all_to_all(send.reshape(peers, 8, tok), "ctx", 0, 0)
    back = pl.pallas_call(
        convolve_kernel,
        grid_spec=pltpu.PrefetchScalarGridSpec(
            num_scalar_prefetch=3,
            grid=(1,),
            in_specs=[whole((peers, 8, tok)), whole((pairs, 2 * BLK, 2 * BLK))],
            out_specs=whole((peers, 8, tok + BLK)),
            scratch_shapes=[
                pltpu.VMEM((blocks * 8, 2 * BLK), BF16),
                pltpu.VMEM((2 * pairs, blocks + CHUNK, 8, BLK), F32),
                pltpu.VMEM((blocks, 8, BLK), F32),
                pltpu.VMEM((2 * blocks, 8, BLK), F32),
                pltpu.VMEM((2, blocks, 8, BLK), F32),
                pltpu.VMEM((2 * BLK, blocks * 8), BF16),
                pltpu.VMEM((stored, BLK, BLK), F32),
                pltpu.VMEM((stored, 8, span), F32),
            ],
        ),
        out_shape=jax.ShapeDtypeStruct((peers, 8, tok + BLK), BF16),
        compiler_params=params(24),
        cost_estimate=cost(pairs * 16 * blocks * 8 * BLK * BLK, peers * 32 * tok),
        name="convolve",
    )(group, lag_blocks, filter_ids, seen, rhs)
    got = lax.all_to_all(back, "ctx", 0, 0)
    wide = lax.axis_size("ch")
    piece = pl.pallas_call(
        spread_kernel,
        grid=(1,),
        in_specs=[pl.BlockSpec((peers, 8, BLK), lambda i: (0, 0, tok // BLK))],
        out_specs=whole((wide, 8, BLK)),
        out_shape=jax.ShapeDtypeStruct((wide, 8, BLK), BF16),
        compiler_params=params(4),
        name="spread",
    )(got)
    tables = lax.all_to_all(piece, "ch", 0, 0)
    chunk = 2
    rows = 3 * chan
    lines = peers // LINE
    half = LINE // chunk
    extra = -(-groups // 8) * 8 * (stored // LINE)
    gated, partial = pl.pallas_call(
        weights_kernel,
        grid=(peers // chunk,),
        in_specs=[
            whole((chan // 8, 2, 8, tok + BLK)),
            whole((rows, tok)),
            whole((chan, tok)),
            pl.BlockSpec((tok, chunk * share), lambda i: (0, i)),
        ],
        out_specs=[
            whole((chan, tok)),
            pl.BlockSpec((chunk, rows, share), lambda i: (i % half, i // half, 0)),
        ],
        out_shape=[
            jax.ShapeDtypeStruct((chan, tok), BF16),
            jax.ShapeDtypeStruct((LINE, lines * rows + extra, share), BF16),
        ],
        scratch_shapes=[pltpu.VMEM((rows, tok), BF16)],
        compiler_params=params(20),
        cost_estimate=cost(6 * chan * depth * tok, 2 * depth * (tok + 6 * chan)),
        name="weights",
    )(got.reshape(chan // 8, 2, 8, tok + BLK), proj, grad_out, tokens_in)
    partial = pl.pallas_call(
        append_kernel,
        grid=(1,),
        in_specs=[whole((wide, 8, BLK)), pl.BlockSpec(memory_space=pl.ANY)],
        out_specs=pl.BlockSpec((LINE, extra, share), lambda i: (0, lines * rows // extra, 0)),
        out_shape=jax.ShapeDtypeStruct(partial.shape, BF16),
        scratch_shapes=[pltpu.VMEM((groups, 8, BLK), F32)],
        input_output_aliases={1: 0},
        compiler_params=params(8),
        name="append",
    )(tables, partial)
    along_x = [[y * LINE + x for x in range(LINE)] for y in range(lines)]
    along_y = [[y * LINE + x for y in range(lines)] for x in range(LINE)]
    parts = lax.all_to_all(partial, "ctx", 0, 0, axis_index_groups=along_x)
    folded, filter_grad = pl.pallas_call(
        fold_kernel,
        grid=(1,),
        in_specs=[whole(parts.shape)],
        out_specs=[whole((lines, rows, share)), whole((groups, stored, share))],
        out_shape=[
            jax.ShapeDtypeStruct((lines, rows, share), BF16),
            jax.ShapeDtypeStruct((groups, stored, share), F32),
        ],
        compiler_params=params(12),
        name="fold",
    )(parts)
    sums = lax.all_to_all(folded, "ctx", 0, 0, axis_index_groups=along_y)
    w_grad = jnp.sum(sums.astype(F32), axis=0)
    w_grad = jnp.transpose(w_grad.reshape(3, chan, share), (2, 0, 1))
    return gated, w_grad, filter_grad


def solution(mesh):
    placed = (P("ctx", None), P(None, None, "ch"), P(), P(), P(), P("ch", "ctx"))
    return jax.shard_map(
        local,
        mesh=mesh,
        in_specs=placed,
        out_specs=(P("ch", "ctx"), P("ctx", None, "ch"), P()),
        check_vma=False,
    )
```

```python
import jax
import jax.numpy as jnp
from jax import lax
from jax.experimental import pallas as pl
from jax.experimental.pallas import tpu as pltpu
from jax.sharding import PartitionSpec as P

BLK = 128
CHUNK = 24
LINE = 4
HALF = 4
BF16, F32 = jnp.bfloat16, jnp.float32


def low_rows(shape):
    return lax.broadcasted_iota(jnp.int32, shape, len(shape) - 2) < HALF


def project_kernel(w_ref, tok_ref, cot_ref, proj_ref, send_ref, acc):
    chan, tok = cot_ref.shape
    step = pl.program_id(0)
    part = lax.dot_general(
        w_ref[...], tok_ref[...], (((1,), (1,)), ((), ())), preferred_element_type=F32
    )

    @pl.when(step == 0)
    def _():
        acc[...] = part

    @pl.when(step > 0)
    def _():
        acc[...] += part

    @pl.when(step == pl.num_programs(0) - 1)
    def _():
        proj = acc[...].astype(BF16)
        proj_ref[...] = proj
        wide = proj.astype(F32)
        mixed = wide[chan : 2 * chan] * wide[2 * chan :]
        grad_conv = cot_ref[...].astype(F32) * wide[:chan]
        mixed = mixed.reshape(chan // 8, 8, tok)
        grad_conv = grad_conv.reshape(chan // 8, 8, tok)
        low = low_rows(mixed.shape)
        send_ref[:, 0] = jnp.where(low, mixed, pltpu.roll(grad_conv, HALF, 1)).astype(BF16)
        send_ref[:, 1] = jnp.where(low, pltpu.roll(mixed, HALF, 1), grad_conv).astype(BF16)


def matrices_kernel(group_ref, ids_ref, bank_ref, rhs_ref, bank_f32):
    stored = bank_ref.shape[1]
    bank_f32[...] = bank_ref[0].astype(F32)
    first = ids_ref[group_ref[0], 0]
    row = lax.broadcasted_iota(jnp.int32, (BLK, BLK), 0)
    col = lax.broadcasted_iota(jnp.int32, (BLK, BLK), 1)
    rhs_ref[stored // 2, :, BLK:] = jnp.zeros((2 * BLK, BLK), BF16)
    for f in range(stored + 1):
        taps = bank_f32[pl.ds(first if f == stored else f, 1), :]
        rows = jnp.broadcast_to(taps, (BLK, 2 * BLK))
        turned = pltpu.roll(rows, BLK, 1, stride=1, stride_axis=0)[:, :BLK]
        if f == stored:
            turned = jnp.where(col >= row, turned, 0.0)
        lanes = slice((f % 2) * BLK, (f % 2 + 1) * BLK)
        rhs_ref[f // 2, :BLK, lanes] = turned.astype(BF16)
        rhs_ref[f // 2, BLK:, lanes] = turned.T.astype(BF16)


def convolve_kernel(
    group_ref, lags_ref, ids_ref, x_ref, rhs_ref, out_ref, lhs, prod, res, *scratch
):
    conv_part(group_ref, lags_ref, ids_ref, x_ref, rhs_ref, out_ref, lhs, prod, res)
    filter_part(group_ref, lags_ref, ids_ref, x_ref, out_ref, *scratch)


def conv_part(group_ref, lags_ref, ids_ref, x_ref, rhs_ref, out_ref, lhs, prod, res):
    peers, _, tok = x_ref.shape
    per = tok // BLK
    blocks = peers * per
    pairs = rhs_ref.shape[0]
    stored = 2 * (pairs - 1)
    entries = lags_ref.shape[1]
    group = group_ref[0]
    low = low_rows((8, BLK))
    zero = jnp.zeros((8, BLK), F32)

    def tile(i):
        return x_ref[i // per, :, (i % per) * BLK : (i % per + 1) * BLK].astype(F32)

    for i in range(0, blocks, 2):
        left = [jnp.where(low, tile(i + j), zero) for j in (0, 1)]
        right = [jnp.where(low, zero, tile(blocks - 1 - i - j)) for j in (0, 1)]
        lhs[i * 8 : i * 8 + 16, :BLK] = jnp.concatenate(left, 0).astype(BF16)
        lhs[i * 8 : i * 8 + 16, BLK:] = jnp.concatenate(right, 0).astype(BF16)

    def product(pair, carry):
        both = jnp.dot(lhs[...], rhs_ref[pair], preferred_element_type=F32)
        for j in (0, 1):
            half = both[:, j * BLK : (j + 1) * BLK].reshape(blocks, 8, BLK)
            prod[2 * pair + j, CHUNK:] = half
            prod[2 * pair + j, :CHUNK] = jnp.zeros((CHUNK, 8, BLK), F32)
        return carry

    lax.fori_loop(0, pairs, product, 0, unroll=True)
    for start in range(0, blocks, CHUNK):

        def add(k, acc):
            first = jnp.maximum(CHUNK + start - lags_ref[group, k], 0)
            return acc + prod[ids_ref[group, k], pl.ds(first, CHUNK)]

        acc = prod[stored, CHUNK + start : 2 * CHUNK + start]
        res[start : start + CHUNK] = lax.fori_loop(1, entries, add, acc, unroll=True)
    for i in range(blocks):
        both = jnp.where(low, res[i], res[blocks - 1 - i])
        out_ref[i // per, :, (i % per) * BLK : (i % per + 1) * BLK] = both.astype(BF16)


def filter_part(group_ref, lags_ref, ids_ref, x_ref, out_ref, padded, cots, turned, sums, folded):
    peers, _, tok = x_ref.shape
    per = tok // BLK
    blocks = peers * per
    entries = lags_ref.shape[1]
    stored = sums.shape[0]
    group = group_ref[0]
    low = low_rows((8, BLK))
    padded[:blocks] = jnp.zeros((blocks, 8, BLK), F32)
    for i in range(blocks):
        tile = x_ref[i // per, :, (i % per) * BLK : (i % per + 1) * BLK].astype(F32)
        other = pltpu.roll(tile, HALF, 0)
        padded[blocks + i] = jnp.where(low, tile, other)
        cots[0, i] = jnp.where(low, other, 0.0)
        cots[1, i] = jnp.where(low, 0.0, tile)
    step = BLK // 8
    for h in (0, 1):
        for j in range(blocks // step):
            rows = cots[h, j * step : (j + 1) * step].reshape(BLK, BLK)
            turned[h * BLK : (h + 1) * BLK, j * BLK : (j + 1) * BLK] = rows.T.astype(BF16)
    sums[...] = jnp.zeros(sums.shape, F32)
    row = lax.broadcasted_iota(jnp.int32, (BLK, BLK), 0)
    col = lax.broadcasted_iota(jnp.int32, (BLK, BLK), 1)
    low_all = low_rows((blocks, 8, BLK))

    def four(p, carry):
        sides = []
        for j in (0, 2):
            top, bottom = (padded[pl.ds(blocks - lags_ref[group, 4 * p + j + h], blocks)] for h in (0, 1))
            sides.append(jnp.where(low_all, top, bottom).reshape(blocks * 8, BLK).astype(BF16))
        both = jnp.dot(turned[...], jnp.concatenate(sides, 1), preferred_element_type=F32)
        keep = (row >= col) | (p > 0)
        for j in range(4):
            part = both[(j % 2) * BLK : (j % 2 + 1) * BLK, (j // 2) * BLK : (j // 2 + 1) * BLK]
            sums[ids_ref[group, 4 * p + j]] += jnp.where(keep, part, 0.0) if j == 0 else part
        return carry

    lax.fori_loop(0, entries // 4, four, 0, unroll=True)
    for f in range(stored):
        mat = jnp.concatenate([jnp.zeros((BLK, BLK), F32), sums[f].T], 1)
        total = mat[:8]
        for q in range(1, BLK // 8):
            total += pltpu.roll(mat[8 * q : 8 * q + 8], 2 * BLK - 8 * q, 1)
        folded[f] = total
    total = folded[:, 0]
    for s in range(1, 8):
        total += pltpu.roll(folded[:, s], 2 * BLK - s, 1)
    sub = lax.broadcasted_iota(jnp.int32, (8, BLK), 0)
    per_line = stored * LINE // peers
    for y in range(peers // LINE):
        piece = jnp.zeros((8, BLK), F32)
        for r in range(2 * per_line):
            f = y * per_line + r // 2
            piece = jnp.where(sub == r, total[f : f + 1, (r % 2) * BLK : (r % 2 + 1) * BLK], piece)
        for p in range(y * LINE, (y + 1) * LINE):
            out_ref[p, :, tok:] = piece.astype(BF16)


def grads_kernel(back_ref, proj_ref, cot_ref, gated_ref, grads):
    chan, tok = cot_ref.shape
    even = back_ref[:, 0, :, :tok].astype(F32)
    odd = back_ref[:, 1, :, :tok].astype(F32)
    low = low_rows(even.shape)
    conv_out = jnp.where(low, even, pltpu.roll(odd, HALF, 1)).reshape(chan, tok)
    grad_mixed = jnp.where(low, pltpu.roll(even, HALF, 1), odd).reshape(chan, tok)
    gated_ref[...] = (proj_ref[:chan].astype(F32) * conv_out).astype(BF16)
    grads[:chan] = (cot_ref[...].astype(F32) * conv_out).astype(BF16)
    grads[chan : 2 * chan] = (grad_mixed * proj_ref[2 * chan :].astype(F32)).astype(BF16)
    grads[2 * chan :] = (grad_mixed * proj_ref[chan : 2 * chan].astype(F32)).astype(BF16)


def weights_kernel(_, grads_ref, tok_ref, out_ref):
    out_ref[0] = jnp.dot(grads_ref[...], tok_ref[...], preferred_element_type=F32).astype(BF16)


def spread_kernel(back_ref, out_ref):
    both = jnp.sum(back_ref[...].astype(F32), axis=0)
    out_ref[...] = jnp.broadcast_to(both.astype(BF16)[None], out_ref.shape)


def fold_kernel(own_ref, a_ref, b_ref, c_ref, got_ref, out_ref, held):
    lines, rows = own_ref.shape[:2]
    for y in range(lines):
        total = own_ref[y].astype(F32) + a_ref[y].astype(F32)
        total += b_ref[y].astype(F32) + c_ref[y].astype(F32)
        out_ref[y, :rows] = total.astype(BF16)
    groups = held.shape[0]
    both = got_ref[...].astype(F32)
    held[...] = jnp.sum(both.reshape(groups, -1, *both.shape[1:]), axis=1)
    per_line = held.shape[1] // 2
    for j in range(per_line):
        part = jnp.concatenate([held[:, 2 * j], held[:, 2 * j + 1]], axis=1).astype(BF16)
        start = rows + j * groups
        for y in range(lines):
            out_ref[y, start : start + groups] = part


def finish_kernel(got_ref, w_ref, table_ref):
    rows = w_ref.shape[0]
    total = got_ref[0, :rows].astype(F32)
    for y in range(1, got_ref.shape[0]):
        total += got_ref[y, :rows].astype(F32)
    w_ref[...] = total
    groups, stored = table_ref.shape[:2]
    per_line = stored // got_ref.shape[0]
    for f in range(stored):
        start = rows + (f % per_line) * groups
        table_ref[:, f] = got_ref[f // per_line, start : start + groups].astype(F32)


def whole(shape):
    return pl.BlockSpec(shape, lambda *_: (0,) * len(shape))


def params(mib):
    return pltpu.CompilerParams(vmem_limit_bytes=mib << 20)


def cost(flops, moved):
    return pl.CostEstimate(flops=flops, bytes_accessed=moved, transcendentals=0)


def local(tokens_in, w_in, filter_bank, lag_blocks, filter_ids, grad_out):
    chan, tok = grad_out.shape
    depth = tokens_in.shape[1]
    peers = lax.axis_size("ctx")
    blocks = tok * peers // BLK
    groups, stored, span = filter_bank.shape
    entries = lag_blocks.shape[1]
    share = depth // peers
    pairs = stored // 2 + 1
    group = (lax.axis_index("ch") // (lax.axis_size("ch") // groups)).astype(jnp.int32)[None]
    weights = jnp.transpose(w_in, (1, 2, 0)).reshape(3 * chan, depth)
    weights = pltpu.with_memory_space_constraint(weights, pltpu.HBM)
    tokens_in = pltpu.with_memory_space_constraint(tokens_in, pltpu.HBM)
    grad_out = pltpu.with_memory_space_constraint(grad_out, pltpu.HBM)

    deep = depth // 4
    proj, send = pl.pallas_call(
        project_kernel,
        grid=(depth // deep,),
        in_specs=[
            pl.BlockSpec((3 * chan, deep), lambda i: (0, i)),
            pl.BlockSpec((tok, deep), lambda i: (0, i)),
            whole((chan, tok)),
        ],
        out_specs=[whole((3 * chan, tok)), whole((chan // 8, 2, 8, tok))],
        scratch_shapes=[pltpu.VMEM((3 * chan, tok), F32)],
        out_shape=[
            jax.ShapeDtypeStruct((3 * chan, tok), BF16),
            jax.ShapeDtypeStruct((chan // 8, 2, 8, tok), BF16),
        ],
        compiler_params=params(20),
        cost_estimate=cost(6 * chan * depth * tok, 2 * depth * (tok + 3 * chan)),
        name="project",
    )(weights, tokens_in, grad_out)
    rhs = pl.pallas_call(
        matrices_kernel,
        grid_spec=pltpu.PrefetchScalarGridSpec(
            num_scalar_prefetch=2,
            grid=(1,),
            in_specs=[pl.BlockSpec((1, stored, span), lambda i, g, ids: (g[0], 0, 0))],
            out_specs=whole((pairs, 2 * BLK, 2 * BLK)),
            scratch_shapes=[pltpu.VMEM((stored, span), F32)],
        ),
        out_shape=jax.ShapeDtypeStruct((pairs, 2 * BLK, 2 * BLK), BF16),
        compiler_params=params(8),
        cost_estimate=cost(pairs * 40 * BLK * BLK, pairs * 8 * BLK * BLK),
        name="matrices",
    )(group, filter_ids, filter_bank)
    seen = lax.all_to_all(send.reshape(peers, 8, tok), "ctx", 0, 0)
    back = pl.pallas_call(
        convolve_kernel,
        grid_spec=pltpu.PrefetchScalarGridSpec(
            num_scalar_prefetch=3,
            grid=(1,),
            in_specs=[whole((peers, 8, tok)), whole((pairs, 2 * BLK, 2 * BLK))],
            out_specs=whole((peers, 8, tok + BLK)),
            scratch_shapes=[
                pltpu.VMEM((blocks * 8, 2 * BLK), BF16),
                pltpu.VMEM((2 * pairs, blocks + CHUNK, 8, BLK), F32),
                pltpu.VMEM((blocks, 8, BLK), F32),
                pltpu.VMEM((2 * blocks, 8, BLK), F32),
                pltpu.VMEM((2, blocks, 8, BLK), F32),
                pltpu.VMEM((2 * BLK, blocks * 8), BF16),
                pltpu.VMEM((stored, BLK, BLK), F32),
                pltpu.VMEM((stored, 8, span), F32),
            ],
        ),
        out_shape=jax.ShapeDtypeStruct((peers, 8, tok + BLK), BF16),
        compiler_params=params(24),
        cost_estimate=cost(pairs * 16 * blocks * 8 * BLK * BLK, peers * 32 * tok),
        name="convolve",
    )(group, lag_blocks, filter_ids, seen, rhs)
    got = lax.all_to_all(back, "ctx", 0, 0)
    wide = lax.axis_size("ch")
    piece = pl.pallas_call(
        spread_kernel,
        grid=(1,),
        in_specs=[pl.BlockSpec((peers, 8, BLK), lambda i: (0, 0, tok // BLK))],
        out_specs=whole((wide, 8, BLK)),
        out_shape=jax.ShapeDtypeStruct((wide, 8, BLK), BF16),
        compiler_params=params(4),
        name="spread",
    )(got)
    tables = lax.all_to_all(piece, "ch", 0, 0)
    rows = 3 * chan
    lines = peers // LINE
    gated, grads = pl.pallas_call(
        grads_kernel,
        grid=(1,),
        in_specs=[whole((chan // 8, 2, 8, tok + BLK)), whole((rows, tok)), whole((chan, tok))],
        out_specs=[whole((chan, tok)), whole((rows, tok))],
        out_shape=[
            jax.ShapeDtypeStruct((chan, tok), BF16),
            jax.ShapeDtypeStruct((rows, tok), BF16),
        ],
        compiler_params=params(8),
        cost_estimate=cost(8 * rows * tok, 8 * rows * tok),
        name="grads",
    )(got.reshape(chan // 8, 2, 8, tok + BLK), proj, grad_out)
    place = lax.rem(lax.axis_index("ctx"), LINE)

    def part(offset):
        dest = lax.rem(place + offset, LINE).astype(jnp.int32)[None]
        return pl.pallas_call(
            weights_kernel,
            grid_spec=pltpu.PrefetchScalarGridSpec(
                num_scalar_prefetch=1,
                grid=(lines,),
                in_specs=[
                    whole((rows, tok)),
                    pl.BlockSpec((tok, share), lambda i, x: (0, i * LINE + x[0])),
                ],
                out_specs=pl.BlockSpec((1, rows, share), lambda i, x: (i, 0, 0)),
            ),
            out_shape=jax.ShapeDtypeStruct((lines, rows, share), BF16),
            compiler_params=params(8),
            cost_estimate=cost(2 * rows * lines * share * tok, 2 * lines * share * (tok + rows)),
            name="weights",
        )(dest, grads, tokens_in)

    def sent(offset):
        pairs_of = [
            (c, c // LINE * LINE + (c % LINE + offset) % LINE) for c in range(peers)
        ]
        return lax.ppermute(part(offset), "ctx", pairs_of)

    others = [sent(offset) for offset in (2, 1, 3)]
    own = part(0)
    extra = groups * (stored // lines)
    folded = pl.pallas_call(
        fold_kernel,
        grid=(1,),
        in_specs=[whole(own.shape)] * 4 + [whole(tables.shape)],
        out_specs=whole((lines, rows + extra, share)),
        out_shape=jax.ShapeDtypeStruct((lines, rows + extra, share), BF16),
        scratch_shapes=[pltpu.VMEM((groups, 8, BLK), F32)],
        compiler_params=params(12),
        name="fold",
    )(own, *others, tables)
    along_y = [[y * LINE + x for y in range(lines)] for x in range(LINE)]
    sums = lax.all_to_all(folded, "ctx", 0, 0, axis_index_groups=along_y)
    w_grad, filter_grad = pl.pallas_call(
        finish_kernel,
        grid=(1,),
        in_specs=[whole(sums.shape)],
        out_specs=[whole((rows, share)), whole((groups, stored, share))],
        out_shape=[
            jax.ShapeDtypeStruct((rows, share), F32),
            jax.ShapeDtypeStruct((groups, stored, share), F32),
        ],
        compiler_params=params(8),
        name="finish",
    )(sums)
    w_grad = jnp.transpose(w_grad.reshape(3, chan, share), (2, 0, 1))
    return gated, w_grad, filter_grad


def solution(mesh):
    placed = (P("ctx", None), P(None, None, "ch"), P(), P(), P(), P("ch", "ctx"))
    return jax.shard_map(
        local,
        mesh=mesh,
        in_specs=placed,
        out_specs=(P("ch", "ctx"), P("ctx", None, "ch"), P()),
        check_vma=False,
    )
```
